32 devices in a mesh: pipe: 8 (over y, x, core), dp: 4 (over z).
Axes of the slice: x: 2, y: 2, z: 4, core: 2. Of those that a mesh axis runs over, the one named last changes fastest.
Arguments:
- inputs: bfloat16 [8, 1024, 1024], P('pipe', 'dp'), may hold values from -6 to 6
- cotangents: bfloat16 [8, 1024, 512], P('pipe', 'dp'), may hold values from -0.09375 to 0.09375
- input_factors: float32 [8, 1024, 256], P('pipe', 'dp'), may hold values from -20 to 20, as said below
- output_factors: float32 [8, 512, 512], P('pipe'), may hold values from -20 to 20, as said below
- input_coupling: float32 [8, 1024, 256], P('pipe', 'dp'), may hold values from -0.375 to 0.375
- output_coupling: float32 [8, 512, 512], P('pipe'), may hold values from -0.25 to 0.25
Outputs:
- update: float32 [8, 1024, 512], P('pipe', 'dp')
The draws below stay inside these ranges and needn't reach their ends.
Inputs may be any that keep to these rules, and one draw needn't show every extreme that they name: Each [256, 256] row block of a layer's input_factors is positive definite. Each layer's output_factors is positive definite.
All inputs are finite; a program needn't handle non-finite values. Where the reference program divides by a largest or mean magnitude, that divisor is 1e-20 or more.
Results may differ from the reference program's by a relative error of at most 0.0003.
Values may be sent and summed in bfloat16 or wider, within the bound.
A program may use at most 64 MiB of HBM per device.

```python
import math
import jax
import jax.numpy as jnp
from jax import lax

BLOCK = 256
OUTC = 512
NS_ITERS = 2
LAYERS = 8
PANEL = 1024
TOKENS = 1024


def factor_block(key, order):
    key_noise, key_spread = jax.random.split(key)
    samples = jax.random.normal(key_noise, (order, 4 * order), jnp.float32)
    spread = jnp.exp(jax.random.uniform(key_spread, (order,), jnp.float32, 0.0, math.log(3.0)))
    product = jnp.dot(samples, samples.T, precision=lax.Precision.HIGHEST) / (4.0 * order)
    return spread[:, None] * product * spread[None, :]


def input_block(key):
    return factor_block(key, BLOCK)


def output_block(key):
    return factor_block(key, OUTC)


def draw_input_factors(key, part):
    block_count = LAYERS * (PANEL // BLOCK)
    key_list = jax.random.split(jax.random.fold_in(key, 11), block_count)
    stacked = lax.map(input_block, key_list)
    return stacked.reshape(LAYERS, PANEL, BLOCK)


def draw_output_factors(key, part):
    key_list = jax.random.split(jax.random.fold_in(key, 23), LAYERS)
    return lax.map(output_block, key_list)


def strengthened(values, key, source, target, blocks, factor):
    def block_of(axis_at):
        return (jnp.arange(values.shape[axis_at]) // (values.shape[axis_at] // blocks)).reshape((-1,) + (1,) * (values.ndim - 1 - axis_at))

    near = jax.random.permutation(key, blocks)[block_of(target)]
    other_side = (block_of(target) + blocks // 2) % blocks
    return jnp.where((block_of(source) == near) | (block_of(source) == other_side), factor * values, values)


def block_scale(rng, shape, shards, smallest, high):
    factor_of, own = 1.0, jax.random.fold_in(rng, 6)
    for dim, parts in shards:
        steps = jnp.exp(jax.random.uniform(jax.random.fold_in(own, dim), (parts,), jnp.float32, smallest / len(shards), high / len(shards)))
        factor_of = factor_of * jnp.repeat(steps, shape[dim] // parts).reshape([-1 if axis == dim else 1 for axis in range(len(shape))])
    return factor_of


def noise(rng, shape, width, reach, cuts=(), kind=jnp.bfloat16):
    array = width * jax.random.normal(rng, shape, jnp.float32)
    if cuts:
        array = array * block_scale(rng, shape, cuts, -0.22, 0.18)
    return jnp.clip(array, -reach, reach).astype(kind)


def heavy_noise(key, dims, scale, bound, cuts, heavy, kind=jnp.bfloat16):
    array = scale * jax.random.normal(key, dims, jnp.float32)
    if cuts:
        array = array * block_scale(key, dims, cuts, -0.22, 0.18)
    return jnp.clip(strengthened(array, jax.random.fold_in(key, 3), *heavy), -bound, bound).astype(kind)


def setup_inputs(seed: int = 0) -> dict:
    streams_of = jax.random.split(jax.random.key(seed), 7)
    inputs = heavy_noise(streams_of[0], (LAYERS, TOKENS, PANEL), 1.0, 6.0, ((0, 8), (1, 4)), (1, 2, 4, 2.0))
    cotangents = noise(streams_of[1], (LAYERS, TOKENS, OUTC), 0.015625, 0.09375, ((0, 8), (1, 4)))
    input_factors = draw_input_factors(jax.random.fold_in(streams_of[6], 71), 0)
    output_factors = draw_output_factors(jax.random.fold_in(streams_of[6], 71), 0)
    input_coupling = noise(streams_of[4], (LAYERS, PANEL, BLOCK), BLOCK ** -0.5, 0.375, ((0, 8), (1, 4)), jnp.float32)
    output_coupling = noise(streams_of[5], (LAYERS, OUTC, OUTC), OUTC ** -0.5, 0.25, ((0, 8),), jnp.float32)
    return dict(inputs=inputs, cotangents=cotangents, input_factors=input_factors, output_factors=output_factors, input_coupling=input_coupling, output_coupling=output_coupling)


def matmul(left, right):
    return jnp.matmul(left, right, precision=lax.Precision.HIGHEST)


def invert(factor):
    order = factor.shape[-1]
    identity = jnp.eye(order, dtype=jnp.float32)
    bound_value = jnp.max(jnp.sum(jnp.abs(factor), axis=1))
    iterate = identity / bound_value
    for sweep in range(NS_ITERS):
        iterate = matmul(iterate, 2.0 * identity - matmul(factor, iterate))
    return iterate


def layer_gradient(pair):
    activations, cotangent_block = pair
    return lax.dot_general(activations, cotangent_block, (((0,), (0,)), ((), ())), preferred_element_type=jnp.float32)


def reference(inputs, cotangents, input_factors, output_factors, input_coupling, output_coupling):
    blocks = PANEL // BLOCK
    gradient = lax.map(layer_gradient, (inputs, cotangents))
    gradient = gradient.reshape(LAYERS, blocks, BLOCK, OUTC)
    factor_blocks = input_factors.reshape(LAYERS, blocks, BLOCK, BLOCK)
    coupling_blocks = input_coupling.reshape(LAYERS, blocks, BLOCK, BLOCK)
    input_inverse = lax.map(jax.vmap(invert), factor_blocks)
    output_inverse = lax.map(invert, output_factors)
    highest = lax.Precision.HIGHEST
    following = jnp.concatenate([gradient[1:], jnp.zeros_like(gradient[:1])], axis=0)
    mixed = jnp.einsum("lbij,lbjk->lbik", coupling_blocks, following, precision=highest)
    mixed = jnp.einsum("lbik,lmk->lbim", mixed, output_coupling, precision=highest)
    coupled = gradient - mixed
    scaled = jnp.einsum("lbij,lbjk->lbik", input_inverse, coupled, precision=highest)
    scaled = jnp.einsum("lbik,lkm->lbim", scaled, output_inverse, precision=highest)
    carried = jnp.einsum("lbji,lbjk->lbik", coupling_blocks, scaled, precision=highest)
    carried = jnp.einsum("lbik,lkm->lbim", carried, output_coupling, precision=highest)
    earlier = jnp.concatenate([jnp.zeros_like(carried[:1]), carried[:-1]], axis=0)
    update = scaled - earlier
    return update.reshape(LAYERS, PANEL, OUTC)
```

```python
import functools

import jax
import jax.numpy as jnp
from jax import lax
from jax.experimental import pallas as pl
from jax.experimental.pallas import tpu as pltpu
from jax.sharding import PartitionSpec as P

MESH = pl.DeviceIdType.MESH
F32 = jnp.float32
BF16 = jnp.bfloat16
WIDTH = 128


def split(value):
    high = value.astype(BF16)
    return high, (value - high.astype(F32)).astype(BF16)


def dot(left, right):
    return jnp.dot(left, right, preferred_element_type=F32)


def dot3(left, right):
    (lh, ll), (rh, rl) = left, right
    return dot(lh, rh) + (dot(lh, rl) + dot(ll, rh))


def invert(factor):
    order = factor.shape[-1]
    bound = jnp.max(jnp.sum(jnp.abs(factor), axis=1, keepdims=True))
    scaled = factor / bound
    rows = lax.broadcasted_iota(jnp.int32, (order, order), 0)
    cols = lax.broadcasted_iota(jnp.int32, (order, order), 1)
    four = jnp.where(rows == cols, jnp.float32(4.0), jnp.float32(0.0))
    parts = split(scaled)
    square = dot3(parts, parts)
    cubic = dot3(split(square), split(four - scaled))
    return (four - 6.0 * scaled + cubic) / bound


def kernel(
    layers, n,
    x_ref, c_ref, a_ref, b_ref, p_ref, q_ref,
    out_ref,
    xcols, xt, call, a_v, b_v, p_v, q_v,
    ia, ib, ph, pt, qh, qt,
    grad, follow, mixed, scaled, carried, earlier,
    local_sem, xsend, xrecv, csend, crecv, gsend, grecv, ksend, krecv,
):
    layer, me = lax.axis_index("pipe"), lax.axis_index("dp")
    tokens, block = xcols.shape[1], xcols.shape[2]
    outc = grad.shape[1]
    width = min(WIDTH, outc)
    chunks = outc // width
    has_next, has_prev = layer < layers - 1, layer > 0

    def span(index):
        return pl.ds(index * width, width)

    def columns(index):
        return pl.ds(pl.multiple_of(index * block, block), block)

    locals_ = [
        pltpu.make_async_copy(src, dst, local_sem.at[i])
        for i, (src, dst) in enumerate([
            (b_ref.at[0], b_v), (a_ref.at[0], a_v), (p_ref.at[0], p_v), (q_ref.at[0], q_v),
            (x_ref.at[0, :, columns(me)], xcols.at[me]), (c_ref.at[0], call.at[me]),
        ])
    ]

    barrier = pltpu.get_barrier_semaphore()
    for d in range(1, n):
        pl.semaphore_signal(barrier, inc=1, device_id=(layer, lax.rem(me + d, n)), device_id_type=MESH)

    @pl.when(has_prev)
    def _():
        pl.semaphore_signal(barrier, inc=1, device_id=(layer - 1, me), device_id_type=MESH)

    @pl.when(has_next)
    def _():
        pl.semaphore_signal(barrier, inc=1, device_id=(layer + 1, me), device_id_type=MESH)

    for copy in locals_:
        copy.start()
    pl.semaphore_wait(barrier, n - 1 + has_prev.astype(jnp.int32) + has_next.astype(jnp.int32))

    def x_copy(target):
        return pltpu.make_async_remote_copy(
            src_ref=x_ref.at[0, :, columns(target)], dst_ref=xcols.at[me],
            send_sem=xsend.at[target], recv_sem=xrecv.at[me],
            device_id=(layer, target), device_id_type=MESH)

    def x_arrival(source):
        return pltpu.make_async_remote_copy(
            src_ref=xcols.at[source], dst_ref=xcols.at[source],
            send_sem=xsend.at[source], recv_sem=xrecv.at[source],
            device_id=(layer, source), device_id_type=MESH)

    for d in range(n - 1, 0, -1):
        for target in (me + d, me - d):
            @pl.when((target >= 0) & (target < n))
            def _(target=target):
                x_copy(target).start()

    def c_copy(source, chunk, step, own=False):
        block_ref = call.at[source, :, span(chunk)]
        return pltpu.make_async_remote_copy(
            src_ref=c_ref.at[0, :, span(chunk)] if own else block_ref, dst_ref=block_ref,
            send_sem=csend.at[(step + 1) // 2, source, chunk], recv_sem=crecv.at[source, chunk],
            device_id=(layer, me + step), device_id_type=MESH)

    def can_go(step):
        return me < n - 1 if step > 0 else me > 0

    def send_own(chunk):
        for step in (1, -1):
            @pl.when(can_go(step))
            def _(step=step):
                c_copy(me, chunk, step, True).start()

    def relay(chunk):
        for d in range(1, n):
            for step in (1, -1):
                source = me - step * d

                @pl.when((source >= 0) & (source < n))
                def _(source=source, step=step):
                    c_copy(source, chunk, -step).wait_recv()

                    @pl.when(can_go(step))
                    def _():
                        c_copy(source, chunk, step).start()

    def g_copy(chunk):
        return pltpu.make_async_remote_copy(
            src_ref=grad.at[:, span(chunk)], dst_ref=follow.at[:, span(chunk)],
            send_sem=gsend.at[chunk], recv_sem=grecv.at[chunk],
            device_id=(layer - 1, me), device_id_type=MESH)

    def k_copy(chunk):
        return pltpu.make_async_remote_copy(
            src_ref=carried.at[:, span(chunk)], dst_ref=earlier.at[:, span(chunk)],
            send_sem=ksend.at[chunk], recv_sem=krecv.at[chunk],
            device_id=(layer + 1, me), device_id_type=MESH)

    def put(ref, value):
        ref[0], ref[1] = split(value)

    def both(ref, *index):
        return ref[(0, *index)], ref[(1, *index)]

    send_own(0)

    for copy in locals_:
        copy.wait()
    put(ib, invert(b_v[...]))
    put(ia, invert(a_v[...]))
    put(ph, p_v[...])
    put(pt, p_v[...].T)
    put(qh, q_v[...])
    put(qt, q_v[...].T)
    mixed[...] = jnp.zeros_like(mixed)

    @pl.when(jnp.logical_not(has_next))
    def _():
        follow[...] = jnp.zeros_like(follow)

    @pl.when(jnp.logical_not(has_prev))
    def _():
        earlier[...] = jnp.zeros_like(earlier)

    for source in range(n):
        @pl.when(source != me)
        def _(source=source):
            x_arrival(source).wait_recv()

        xt[:, source * tokens:(source + 1) * tokens] = xcols[source].T

    def mix(chunk):
        @pl.when(has_next)
        def _():
            g_copy(chunk).wait_recv()

        part = dot3(both(ph), split(follow[:, chunk * width:(chunk + 1) * width]))
        mixed[...] += dot3(split(part), both(qt, slice(chunk * width, (chunk + 1) * width)))

    for chunk in range(chunks):
        if chunk + 1 < chunks:
            send_own(chunk + 1)
        relay(chunk)
        right = call[:, :, chunk * width:(chunk + 1) * width].reshape(n * tokens, width)
        grad[:, chunk * width:(chunk + 1) * width] = dot(xt[...], right)

        @pl.when(has_prev)
        def _(chunk=chunk):
            g_copy(chunk).start()

        if chunk > 0:
            mix(chunk - 1)
    mix(chunks - 1)

    coupled = grad[...] - mixed[...]
    half = dot3(both(ia), split(coupled))
    scaled[...] = dot3(split(half), both(ib))
    half = split(dot3(both(pt), split(scaled[...])))
    for chunk in range(chunks):
        carried[:, chunk * width:(chunk + 1) * width] = dot3(
            half, both(qh, slice(None), slice(chunk * width, (chunk + 1) * width)))

        @pl.when(has_next)
        def _(chunk=chunk):
            k_copy(chunk).start()

    for chunk in range(chunks):
        @pl.when(has_prev)
        def _(chunk=chunk):
            k_copy(chunk).wait_recv()

        part = slice(chunk * width, (chunk + 1) * width)
        out_ref[:, part] = scaled[:, part] - earlier[:, part]

    for d in range(n - 1, 0, -1):
        for target in (me + d, me - d):
            @pl.when((target >= 0) & (target < n))
            def _(target=target):
                x_copy(target).wait_send()
    for chunk in range(chunks):
        for step in (1, -1):
            for d in range(n):
                source = me - step * d

                @pl.when((source >= 0) & (source < n) & can_go(step))
                def _(source=source, step=step, chunk=chunk, d=d):
                    c_copy(source, chunk, step, d == 0).wait_send()

        @pl.when(has_prev)
        def _(chunk=chunk):
            g_copy(chunk).wait_send()

        @pl.when(has_next)
        def _(chunk=chunk):
            k_copy(chunk).wait_send()


def shards(layers, n, inputs, cotangents, input_factors, output_factors, input_coupling, output_coupling):
    tokens = inputs.shape[1]
    block = input_factors.shape[2]
    outc = cotangents.shape[2]
    chunks = outc // min(WIDTH, outc)
    dma = pltpu.SemaphoreType.DMA
    panel = pltpu.VMEM((block, outc), F32)
    out = pl.pallas_call(
        functools.partial(kernel, layers, n),
        out_shape=jax.ShapeDtypeStruct((block, outc), F32),
        in_specs=[pl.BlockSpec(memory_space=pl.ANY)] * 6,
        out_specs=pl.BlockSpec(memory_space=pltpu.VMEM),
        scratch_shapes=[
            pltpu.VMEM((n, tokens, block), BF16),
            pltpu.VMEM((block, n * tokens), BF16),
            pltpu.VMEM((n, tokens, outc), BF16),
            pltpu.VMEM((block, block), F32),
            pltpu.VMEM((outc, outc), F32),
            pltpu.VMEM((block, block), F32),
            pltpu.VMEM((outc, outc), F32),
            pltpu.VMEM((2, block, block), BF16),
            pltpu.VMEM((2, outc, outc), BF16),
            pltpu.VMEM((2, block, block), BF16),
            pltpu.VMEM((2, block, block), BF16),
            pltpu.VMEM((2, outc, outc), BF16),
            pltpu.VMEM((2, outc, outc), BF16),
            panel, panel, panel, panel, panel, panel,
            dma((6,)),
            dma((n,)), dma((n,)),
            dma((2, n, chunks)), dma((n, chunks)),
            dma((chunks,)), dma((chunks,)), dma((chunks,)), dma((chunks,)),
        ],
        compiler_params=pltpu.CompilerParams(
            collective_id=0, has_side_effects=True, vmem_limit_bytes=60 * 1024 * 1024),
    )(inputs, cotangents, input_factors, output_factors, input_coupling, output_coupling)
    return out[None]


def solution(mesh):
    in_specs = (
        P("pipe", "dp", None),
        P("pipe", "dp", None),
        P("pipe", "dp", None),
        P("pipe", None, None),
        P("pipe", "dp", None),
        P("pipe", None, None),
    )
    body = functools.partial(shards, mesh.shape["pipe"], mesh.shape["dp"])
    return jax.shard_map(body, mesh=mesh, in_specs=in_specs, out_specs=P("pipe", "dp", None), check_vma=False)
```

```python
import functools

import jax
import jax.numpy as jnp
from jax import lax
from jax.experimental import pallas as pl
from jax.experimental.pallas import tpu as pltpu
from jax.sharding import PartitionSpec as P

MESH = pl.DeviceIdType.MESH
F32 = jnp.float32
BF16 = jnp.bfloat16
WIDTH = 128
LOOKAHEAD = 2


def split(value):
    high = value.astype(BF16)
    return high, (value - high.astype(F32)).astype(BF16)


def dot(left, right):
    return jnp.dot(left, right, preferred_element_type=F32)


def dot3(left, right):
    (lh, ll), (rh, rl) = left, right
    return dot(lh, rh) + (dot(lh, rl) + dot(ll, rh))


def invert(factor):
    order = factor.shape[-1]
    bound = jnp.max(jnp.sum(jnp.abs(factor), axis=1, keepdims=True))
    scaled = factor / bound
    rows = lax.broadcasted_iota(jnp.int32, (order, order), 0)
    cols = lax.broadcasted_iota(jnp.int32, (order, order), 1)
    four = jnp.where(rows == cols, jnp.float32(4.0), jnp.float32(0.0))
    parts = split(scaled)
    square = dot3(parts, parts)
    cubic = dot3(split(square), split(four - scaled))
    return (four - 6.0 * scaled + cubic) / bound


def kernel(
    layers, n,
    x_ref, c_ref, a_ref, b_ref, p_ref, q_ref,
    scaled_ref, earlier_ref,
    xcols, xt, call, a_v, b_v, p_v, q_v,
    ia, ib, ph, pa, bq, qt,
    grad, follow, mixed, scaled, carried,
    local_sem, xsend, xrecv, csend, crecv, gsend, grecv, ksend, krecv,
):
    layer, me = lax.axis_index("pipe"), lax.axis_index("dp")
    tokens, block = xcols.shape[1], xcols.shape[2]
    outc = grad.shape[1]
    width = min(WIDTH, outc)
    chunks = outc // width
    has_next, has_prev = layer < layers - 1, layer > 0

    def span(index):
        return pl.ds(index * width, width)

    def columns(index):
        return pl.ds(pl.multiple_of(index * block, block), block)

    locals_ = [
        pltpu.make_async_copy(src, dst, local_sem.at[i])
        for i, (src, dst) in enumerate([
            (b_ref.at[0], b_v), (a_ref.at[0], a_v), (p_ref.at[0], p_v), (q_ref.at[0], q_v),
            (x_ref.at[0, :, columns(me)], xcols.at[me]), (c_ref.at[0], call.at[me]),
        ])
    ]

    barrier = pltpu.get_barrier_semaphore()
    for d in range(1, n):
        pl.semaphore_signal(barrier, inc=1, device_id=(layer, lax.rem(me + d, n)), device_id_type=MESH)

    @pl.when(has_prev)
    def _():
        pl.semaphore_signal(barrier, inc=1, device_id=(layer - 1, me), device_id_type=MESH)

    @pl.when(has_next)
    def _():
        pl.semaphore_signal(barrier, inc=1, device_id=(layer + 1, me), device_id_type=MESH)

    for copy in locals_:
        copy.start()
    pl.semaphore_wait(barrier, n - 1 + has_prev.astype(jnp.int32) + has_next.astype(jnp.int32))

    def x_copy(target):
        return pltpu.make_async_remote_copy(
            src_ref=x_ref.at[0, :, columns(target)], dst_ref=xcols.at[me],
            send_sem=xsend.at[target], recv_sem=xrecv.at[me],
            device_id=(layer, target), device_id_type=MESH)

    def x_arrival(source):
        return pltpu.make_async_remote_copy(
            src_ref=xcols.at[source], dst_ref=xcols.at[source],
            send_sem=xsend.at[source], recv_sem=xrecv.at[source],
            device_id=(layer, source), device_id_type=MESH)

    for d in range(n - 1, 0, -1):
        for target in (me + d, me - d):
            @pl.when((target >= 0) & (target < n))
            def _(target=target):
                x_copy(target).start()

    def c_copy(source, chunk, step, own=False):
        block_ref = call.at[source, :, span(chunk)]
        return pltpu.make_async_remote_copy(
            src_ref=c_ref.at[0, :, span(chunk)] if own else block_ref, dst_ref=block_ref,
            send_sem=csend.at[(step + 1) // 2, source, chunk], recv_sem=crecv.at[source, chunk],
            device_id=(layer, me + step), device_id_type=MESH)

    def can_go(step):
        return me < n - 1 if step > 0 else me > 0

    def send_own(chunk):
        for step in (1, -1):
            @pl.when(can_go(step))
            def _(step=step):
                c_copy(me, chunk, step, True).start()

    def relay(turn):
        for d in range(1, n):
            chunk = turn - (d - 1)
            if not 0 <= chunk < chunks:
                continue
            for step in (1, -1):
                source = me - step * d

                @pl.when((source >= 0) & (source < n))
                def _(source=source, step=step, chunk=chunk):
                    c_copy(source, chunk, -step).wait_recv()

                    @pl.when(can_go(step))
                    def _():
                        c_copy(source, chunk, step).start()

    def g_copy(chunk):
        return pltpu.make_async_remote_copy(
            src_ref=grad.at[:, span(chunk)], dst_ref=follow.at[:, span(chunk)],
            send_sem=gsend.at[chunk], recv_sem=grecv.at[chunk],
            device_id=(layer - 1, me), device_id_type=MESH)

    def k_copy(chunk):
        return pltpu.make_async_remote_copy(
            src_ref=carried.at[:, span(chunk)], dst_ref=earlier_ref.at[:, span(chunk)],
            send_sem=ksend.at[chunk], recv_sem=krecv.at[chunk],
            device_id=(layer + 1, me), device_id_type=MESH)

    def put(ref, value):
        ref[0], ref[1] = split(value)

    def both(ref, *index):
        return ref[(0, *index)], ref[(1, *index)]

    for chunk in range(min(LOOKAHEAD, chunks)):
        send_own(chunk)

    for copy in locals_:
        copy.wait()
    carried[...] = jnp.zeros_like(carried)
    put(ib, invert(b_v[...]))
    put(ia, invert(a_v[...]))
    put(ph, p_v[...])
    put(qt, q_v[...].T)
    put(pa, dot3(split(p_v[...].T), both(ia)))
    put(bq, dot3(both(ib), split(q_v[...])))

    @pl.when(jnp.logical_not(has_prev))
    def _():
        blank = pltpu.make_async_copy(carried, earlier_ref, local_sem.at[0])
        blank.start()
        blank.wait()

    mixed[...] = jnp.zeros_like(mixed)

    @pl.when(jnp.logical_not(has_next))
    def _():
        follow[...] = jnp.zeros_like(follow)

    for source in range(n):
        @pl.when(source != me)
        def _(source=source):
            x_arrival(source).wait_recv()

        xt[:, source * tokens:(source + 1) * tokens] = xcols[source].T

    def mix(chunk):
        @pl.when(has_next)
        def _():
            g_copy(chunk).wait_recv()

        part = dot3(both(ph), split(follow[:, chunk * width:(chunk + 1) * width]))
        mixed[...] += dot3(split(part), both(qt, slice(chunk * width, (chunk + 1) * width)))

    for turn in range(chunks + n - 2):
        if turn + LOOKAHEAD < chunks:
            send_own(turn + LOOKAHEAD)
        relay(turn)
        chunk = turn - (n - 2)
        if chunk < 0:
            continue
        right = call[:, :, chunk * width:(chunk + 1) * width].reshape(n * tokens, width)
        grad[:, chunk * width:(chunk + 1) * width] = dot(xt[...], right)

        @pl.when(has_prev)
        def _(chunk=chunk):
            g_copy(chunk).start()

        if chunk > 0:
            mix(chunk - 1)
    mix(chunks - 1)

    coupled = split(grad[...] - mixed[...])
    half = split(dot3(both(pa), coupled))
    for chunk in range(chunks):
        carried[:, chunk * width:(chunk + 1) * width] = dot3(
            half, both(bq, slice(None), slice(chunk * width, (chunk + 1) * width)))

        @pl.when(has_next)
        def _(chunk=chunk):
            k_copy(chunk).start()

    scaled[...] = dot3(split(dot3(both(ia), coupled)), both(ib))
    result = pltpu.make_async_copy(scaled, scaled_ref, local_sem.at[0])
    result.start()
    for chunk in range(chunks):
        @pl.when(has_prev)
        def _(chunk=chunk):
            k_copy(chunk).wait_recv()

    result.wait()

    for d in range(n - 1, 0, -1):
        for target in (me + d, me - d):
            @pl.when((target >= 0) & (target < n))
            def _(target=target):
                x_copy(target).wait_send()
    for chunk in range(chunks):
        for step in (1, -1):
            for d in range(n):
                source = me - step * d

                @pl.when((source >= 0) & (source < n) & can_go(step))
                def _(source=source, step=step, chunk=chunk, d=d):
                    c_copy(source, chunk, step, d == 0).wait_send()

        @pl.when(has_prev)
        def _(chunk=chunk):
            g_copy(chunk).wait_send()

        @pl.when(has_next)
        def _(chunk=chunk):
            k_copy(chunk).wait_send()


def shards(layers, n, inputs, cotangents, input_factors, output_factors, input_coupling, output_coupling):
    tokens = inputs.shape[1]
    block = input_factors.shape[2]
    outc = cotangents.shape[2]
    chunks = outc // min(WIDTH, outc)
    dma = pltpu.SemaphoreType.DMA
    panel = pltpu.VMEM((block, outc), F32)
    scaled, earlier = pl.pallas_call(
        functools.partial(kernel, layers, n),
        out_shape=[jax.ShapeDtypeStruct((block, outc), F32)] * 2,
        in_specs=[pl.BlockSpec(memory_space=pl.ANY)] * 6,
        out_specs=[pl.BlockSpec(memory_space=pl.ANY)] * 2,
        scratch_shapes=[
            pltpu.VMEM((n, tokens, block), BF16),
            pltpu.VMEM((block, n * tokens), BF16),
            pltpu.VMEM((n, tokens, outc), BF16),
            pltpu.VMEM((block, block), F32),
            pltpu.VMEM((outc, outc), F32),
            pltpu.VMEM((block, block), F32),
            pltpu.VMEM((outc, outc), F32),
            pltpu.VMEM((2, block, block), BF16),
            pltpu.VMEM((2, outc, outc), BF16),
            pltpu.VMEM((2, block, block), BF16),
            pltpu.VMEM((2, block, block), BF16),
            pltpu.VMEM((2, outc, outc), BF16),
            pltpu.VMEM((2, outc, outc), BF16),
            panel, panel, panel, panel, panel,
            dma((6,)),
            dma((n,)), dma((n,)),
            dma((2, n, chunks)), dma((n, chunks)),
            dma((chunks,)), dma((chunks,)), dma((chunks,)), dma((chunks,)),
        ],
        compiler_params=pltpu.CompilerParams(
            collective_id=0, has_side_effects=True, vmem_limit_bytes=60 * 1024 * 1024),
    )(inputs, cotangents, input_factors, output_factors, input_coupling, output_coupling)
    return (scaled - earlier)[None]


def solution(mesh):
    in_specs = (
        P("pipe", "dp", None),
        P("pipe", "dp", None),
        P("pipe", "dp", None),
        P("pipe", None, None),
        P("pipe", "dp", None),
        P("pipe", None, None),
    )
    body = functools.partial(shards, mesh.shape["pipe"], mesh.shape["dp"])
    return jax.shard_map(body, mesh=mesh, in_specs=in_specs, out_specs=P("pipe", "dp", None), check_vma=False)
```

```python
import functools

import jax
import jax.numpy as jnp
from jax import lax
from jax.experimental import pallas as pl
from jax.experimental.pallas import tpu as pltpu
from jax.sharding import PartitionSpec as P

MESH = pl.DeviceIdType.MESH
F32 = jnp.float32
BF16 = jnp.bfloat16
WIDTH = 128
VMEM = 67043328
LOOKAHEAD = 2


def split(value):
    high = value.astype(BF16)
    return high, (value - high.astype(F32)).astype(BF16)


def dot(left, right):
    return jnp.dot(left, right, preferred_element_type=F32)


def dot3(left, right):
    (lh, ll), (rh, rl) = left, right
    return dot(lh, rh) + (dot(lh, rl) + dot(ll, rh))


def invert(factor):
    order = factor.shape[-1]
    bound = jnp.max(jnp.sum(jnp.abs(factor), axis=1, keepdims=True))
    scaled = factor / bound
    rows = lax.broadcasted_iota(jnp.int32, (order, order), 0)
    cols = lax.broadcasted_iota(jnp.int32, (order, order), 1)
    four = jnp.where(rows == cols, jnp.float32(4.0), jnp.float32(0.0))
    parts = split(scaled)
    square = dot3(parts, parts)
    cubic = dot3(split(square), split(four - scaled))
    return (four - 6.0 * scaled + cubic) / bound


def kernel(
    layers, n,
    x_ref, c_ref, a_ref, b_ref, p_ref, q_ref,
    scaled_ref, earlier_ref,
    xcols, xt, call, a_v, b_v, p_v, q_v,
    ia, ib, ph, pa, bq, qt,
    grad, follow, mixed, carried,
    local_sem, xsend, xrecv, csend, crecv, gsend, grecv, ksend, krecv,
):
    layer, me = lax.axis_index("pipe"), lax.axis_index("dp")
    tokens, block = xcols.shape[1], xcols.shape[2]
    outc = grad.shape[1]
    width = min(WIDTH, outc)
    chunks = outc // width
    has_next, has_prev = layer < layers - 1, layer > 0

    def span(index):
        return pl.ds(index * width, width)

    def columns(index):
        return pl.ds(pl.multiple_of(index * block, block), block)

    locals_ = [
        pltpu.make_async_copy(src, dst, local_sem.at[i])
        for i, (src, dst) in enumerate([
            (b_ref.at[0], b_v), (a_ref.at[0], a_v), (p_ref.at[0], p_v), (q_ref.at[0], q_v),
            (x_ref.at[0, :, columns(me)], xcols.at[me]), (c_ref.at[0], call.at[me]),
        ])
    ]

    barrier = pltpu.get_barrier_semaphore()
    for d in range(1, n):
        pl.semaphore_signal(barrier, inc=1, device_id=(layer, lax.rem(me + d, n)), device_id_type=MESH)

    @pl.when(has_prev)
    def _():
        pl.semaphore_signal(barrier, inc=1, device_id=(layer - 1, me), device_id_type=MESH)

    @pl.when(has_next)
    def _():
        pl.semaphore_signal(barrier, inc=1, device_id=(layer + 1, me), device_id_type=MESH)

    for copy in locals_:
        copy.start()
    pl.semaphore_wait(barrier, n - 1 + has_prev.astype(jnp.int32) + has_next.astype(jnp.int32))

    def x_copy(target):
        return pltpu.make_async_remote_copy(
            src_ref=x_ref.at[0, :, columns(target)], dst_ref=xcols.at[me],
            send_sem=xsend.at[target], recv_sem=xrecv.at[me],
            device_id=(layer, target), device_id_type=MESH)

    def x_arrival(source):
        return pltpu.make_async_remote_copy(
            src_ref=xcols.at[source], dst_ref=xcols.at[source],
            send_sem=xsend.at[source], recv_sem=xrecv.at[source],
            device_id=(layer, source), device_id_type=MESH)

    for d in range(n - 1, 0, -1):
        for target in (me + d, me - d):
            @pl.when((target >= 0) & (target < n))
            def _(target=target):
                x_copy(target).start()

    def c_copy(source, chunk, step, own=False):
        block_ref = call.at[source, :, span(chunk)]
        return pltpu.make_async_remote_copy(
            src_ref=c_ref.at[0, :, span(chunk)] if own else block_ref, dst_ref=block_ref,
            send_sem=csend.at[(step + 1) // 2, source, chunk], recv_sem=crecv.at[source, chunk],
            device_id=(layer, me + step), device_id_type=MESH)

    def can_go(step):
        return me < n - 1 if step > 0 else me > 0

    def send_own(chunk):
        for step in (1, -1):
            @pl.when(can_go(step))
            def _(step=step):
                c_copy(me, chunk, step, True).start()

    def relay(turn):
        for d in range(1, n):
            chunk = turn - (d - 1)
            if not 0 <= chunk < chunks:
                continue
            for step in (1, -1):
                source = me - step * d

                @pl.when((source >= 0) & (source < n))
                def _(source=source, step=step, chunk=chunk):
                    c_copy(source, chunk, -step).wait_recv()

                    @pl.when(can_go(step))
                    def _():
                        c_copy(source, chunk, step).start()

    def g_copy(chunk):
        return pltpu.make_async_remote_copy(
            src_ref=grad.at[:, span(chunk)], dst_ref=follow.at[:, span(chunk)],
            send_sem=gsend.at[chunk], recv_sem=grecv.at[chunk],
            device_id=(layer - 1, me), device_id_type=MESH)

    def k_copy(chunk):
        return pltpu.make_async_remote_copy(
            src_ref=carried.at[:, span(chunk)], dst_ref=earlier_ref.at[:, span(chunk)],
            send_sem=ksend.at[chunk], recv_sem=krecv.at[chunk],
            device_id=(layer + 1, me), device_id_type=MESH)

    def put(ref, value):
        ref[0], ref[1] = split(value)

    def both(ref, *index):
        return ref[(0, *index)], ref[(1, *index)]

    for chunk in range(min(LOOKAHEAD, chunks)):
        send_own(chunk)

    for copy in locals_:
        copy.wait()
    put(ib, invert(b_v[...]))
    put(ia, invert(a_v[...]))
    put(ph, p_v[...])
    put(qt, q_v[...].T)
    put(pa, dot3(split(p_v[...].T), both(ia)))
    put(bq, dot3(both(ib), split(q_v[...])))

    @pl.when(jnp.logical_not(has_prev))
    def _():
        earlier_ref[...] = jnp.zeros_like(earlier_ref)

    mixed[...] = jnp.zeros_like(mixed)

    @pl.when(jnp.logical_not(has_next))
    def _():
        follow[...] = jnp.zeros_like(follow)

    for source in range(n):
        @pl.when(source != me)
        def _(source=source):
            x_arrival(source).wait_recv()

        xt[:, source * tokens:(source + 1) * tokens] = xcols[source].T

    def mix(chunk):
        @pl.when(has_next)
        def _():
            g_copy(chunk).wait_recv()

        part = dot3(both(ph), split(follow[:, chunk * width:(chunk + 1) * width]))
        mixed[...] += dot3(split(part), both(qt, slice(chunk * width, (chunk + 1) * width)))

    for turn in range(chunks + n - 2):
        if turn + LOOKAHEAD < chunks:
            send_own(turn + LOOKAHEAD)
        relay(turn)
        chunk = turn - (n - 2)
        if chunk < 0:
            continue
        right = call[:, :, chunk * width:(chunk + 1) * width].reshape(n * tokens, width)
        grad[:, chunk * width:(chunk + 1) * width] = dot(xt[...], right)

        @pl.when(has_prev)
        def _(chunk=chunk):
            g_copy(chunk).start()

        if chunk > 0:
            mix(chunk - 1)
    mix(chunks - 1)

    coupled = split(grad[...] - mixed[...])
    half = split(dot3(both(pa), coupled))
    for chunk in range(chunks):
        carried[:, chunk * width:(chunk + 1) * width] = dot3(
            half, both(bq, slice(None), slice(chunk * width, (chunk + 1) * width)))

        @pl.when(has_next)
        def _(chunk=chunk):
            k_copy(chunk).start()

    scaled_ref[...] = dot3(split(dot3(both(ia), coupled)), both(ib))
    for chunk in range(chunks):
        @pl.when(has_prev)
        def _(chunk=chunk):
            k_copy(chunk).wait_recv()

    for d in range(n - 1, 0, -1):
        for target in (me + d, me - d):
            @pl.when((target >= 0) & (target < n))
            def _(target=target):
                x_copy(target).wait_send()
    for chunk in range(chunks):
        for step in (1, -1):
            for d in range(n):
                source = me - step * d

                @pl.when((source >= 0) & (source < n) & can_go(step))
                def _(source=source, step=step, chunk=chunk, d=d):
                    c_copy(source, chunk, step, d == 0).wait_send()

        @pl.when(has_prev)
        def _(chunk=chunk):
            g_copy(chunk).wait_send()

        @pl.when(has_next)
        def _(chunk=chunk):
            k_copy(chunk).wait_send()


def shards(layers, n, inputs, cotangents, input_factors, output_factors, input_coupling, output_coupling):
    tokens = inputs.shape[1]
    block = input_factors.shape[2]
    outc = cotangents.shape[2]
    chunks = outc // min(WIDTH, outc)
    dma = pltpu.SemaphoreType.DMA
    panel = pltpu.VMEM((block, outc), F32)
    scaled, earlier = pl.pallas_call(
        functools.partial(kernel, layers, n),
        out_shape=[pltpu.VMEM((block, outc), F32)] * 2,
        in_specs=[pl.BlockSpec(memory_space=pl.ANY)] * 6,
        out_specs=[pl.BlockSpec(memory_space=pltpu.VMEM)] * 2,
        scratch_shapes=[
            pltpu.VMEM((n, tokens, block), BF16),
            pltpu.VMEM((block, n * tokens), BF16),
            pltpu.VMEM((n, tokens, outc), BF16),
            pltpu.VMEM((block, block), F32),
            pltpu.VMEM((outc, outc), F32),
            pltpu.VMEM((block, block), F32),
            pltpu.VMEM((outc, outc), F32),
            pltpu.VMEM((2, block, block), BF16),
            pltpu.VMEM((2, outc, outc), BF16),
            pltpu.VMEM((2, block, block), BF16),
            pltpu.VMEM((2, block, block), BF16),
            pltpu.VMEM((2, outc, outc), BF16),
            pltpu.VMEM((2, outc, outc), BF16),
            panel, panel, panel, panel,
            dma((6,)),
            dma((n,)), dma((n,)),
            dma((2, n, chunks)), dma((n, chunks)),
            dma((chunks,)), dma((chunks,)), dma((chunks,)), dma((chunks,)),
        ],
        compiler_params=pltpu.CompilerParams(
            collective_id=0, has_side_effects=True, vmem_limit_bytes=VMEM - 8 * block * outc - 65536),
    )(inputs, cotangents, input_factors, output_factors, input_coupling, output_coupling)
    return (scaled - earlier)[None]


def solution(mesh):
    in_specs = (
        P("pipe", "dp", None),
        P("pipe", "dp", None),
        P("pipe", "dp", None),
        P("pipe", None, None),
        P("pipe", "dp", None),
        P("pipe", None, None),
    )
    body = functools.partial(shards, mesh.shape["pipe"], mesh.shape["dp"])
    return jax.shard_map(body, mesh=mesh, in_specs=in_specs, out_specs=P("pipe", "dp", None), check_vma=False)
```

```python
import functools

import jax
import jax.numpy as jnp
from jax import lax
from jax.experimental import pallas as pl
from jax.experimental.pallas import tpu as pltpu
from jax.sharding import PartitionSpec as P

MESH = pl.DeviceIdType.MESH
F32 = jnp.float32
BF16 = jnp.bfloat16
WIDTH = 128
VMEM = 67043328
LOOKAHEAD = 2


def split(value):
    high = value.astype(BF16)
    return high, (value - high.astype(F32)).astype(BF16)


def dot(left, right):
    return jnp.dot(left, right, preferred_element_type=F32)


def dot3(left, right):
    (lh, ll), (rh, rl) = left, right
    return dot(lh, rh) + (dot(lh, rl) + dot(ll, rh))


def invert(factor):
    order = factor.shape[-1]
    bound = jnp.max(jnp.sum(jnp.abs(factor), axis=1, keepdims=True))
    scaled = factor / bound
    rows = lax.broadcasted_iota(jnp.int32, (order, order), 0)
    cols = lax.broadcasted_iota(jnp.int32, (order, order), 1)
    four = jnp.where(rows == cols, jnp.float32(4.0), jnp.float32(0.0))
    parts = split(scaled)
    square = dot3(parts, parts)
    cubic = dot3(split(square), split(four - scaled))
    return (four - 6.0 * scaled + cubic) / bound


def kernel(
    layers, n,
    x_ref, c_ref, a_ref, b_ref, p_ref, q_ref,
    scaled_ref, earlier_ref,
    xcols, xt, call, a_v, b_v, p_v, q_v,
    ia, ib, ph, pa, vp, bq, qt, qw,
    grad, follow, mixed, scaled, carried,
    local_sem, xsend, xrecv, csend, crecv, gsend, grecv, ksend, krecv,
):
    layer, me = lax.axis_index("pipe"), lax.axis_index("dp")
    tokens, block = xcols.shape[1], xcols.shape[2]
    outc = grad.shape[1]
    width = min(WIDTH, outc)
    chunks = outc // width
    has_next, has_prev = layer < layers - 1, layer > 0

    def span(index):
        return pl.ds(index * width, width)

    def columns(index):
        return pl.ds(pl.multiple_of(index * block, block), block)

    locals_ = [
        pltpu.make_async_copy(src, dst, local_sem.at[i])
        for i, (src, dst) in enumerate([
            (b_ref.at[0], b_v), (a_ref.at[0], a_v), (p_ref.at[0], p_v), (q_ref.at[0], q_v),
            (x_ref.at[0, :, columns(me)], xcols.at[me]), (c_ref.at[0], call.at[me]),
        ])
    ]

    barrier = pltpu.get_barrier_semaphore()
    for d in range(1, n):
        pl.semaphore_signal(barrier, inc=1, device_id=(layer, lax.rem(me + d, n)), device_id_type=MESH)

    @pl.when(has_prev)
    def _():
        pl.semaphore_signal(barrier, inc=1, device_id=(layer - 1, me), device_id_type=MESH)

    @pl.when(has_next)
    def _():
        pl.semaphore_signal(barrier, inc=1, device_id=(layer + 1, me), device_id_type=MESH)

    for copy in locals_:
        copy.start()
    pl.semaphore_wait(barrier, n - 1 + has_prev.astype(jnp.int32) + has_next.astype(jnp.int32))

    def x_copy(target):
        return pltpu.make_async_remote_copy(
            src_ref=x_ref.at[0, :, columns(target)], dst_ref=xcols.at[me],
            send_sem=xsend.at[target], recv_sem=xrecv.at[me],
            device_id=(layer, target), device_id_type=MESH)

    def x_arrival(source):
        return pltpu.make_async_remote_copy(
            src_ref=xcols.at[source], dst_ref=xcols.at[source],
            send_sem=xsend.at[source], recv_sem=xrecv.at[source],
            device_id=(layer, source), device_id_type=MESH)

    for d in range(n - 1, 0, -1):
        for target in (me + d, me - d):
            @pl.when((target >= 0) & (target < n))
            def _(target=target):
                x_copy(target).start()

    def c_copy(source, chunk, step, own=False):
        block_ref = call.at[source, :, span(chunk)]
        return pltpu.make_async_remote_copy(
            src_ref=c_ref.at[0, :, span(chunk)] if own else block_ref, dst_ref=block_ref,
            send_sem=csend.at[(step + 1) // 2, source, chunk], recv_sem=crecv.at[source, chunk],
            device_id=(layer, me + step), device_id_type=MESH)

    def can_go(step):
        return me < n - 1 if step > 0 else me > 0

    def send_own(chunk):
        for step in (1, -1):
            @pl.when(can_go(step))
            def _(step=step):
                c_copy(me, chunk, step, True).start()

    def relay(turn):
        for d in range(1, n):
            chunk = turn - (d - 1)
            if not 0 <= chunk < chunks:
                continue
            for step in (1, -1):
                source = me - step * d

                @pl.when((source >= 0) & (source < n))
                def _(source=source, step=step, chunk=chunk):
                    c_copy(source, chunk, -step).wait_recv()

                    @pl.when(can_go(step))
                    def _():
                        c_copy(source, chunk, step).start()

    def g_copy(chunk):
        return pltpu.make_async_remote_copy(
            src_ref=grad.at[:, span(chunk)], dst_ref=follow.at[:, span(chunk)],
            send_sem=gsend.at[chunk], recv_sem=grecv.at[chunk],
            device_id=(layer - 1, me), device_id_type=MESH)

    def k_copy(chunk):
        return pltpu.make_async_remote_copy(
            src_ref=carried.at[:, span(chunk)], dst_ref=earlier_ref.at[:, span(chunk)],
            send_sem=ksend.at[chunk], recv_sem=krecv.at[chunk],
            device_id=(layer + 1, me), device_id_type=MESH)

    def put(ref, value):
        ref[0], ref[1] = split(value)

    def both(ref, *index):
        return ref[(0, *index)], ref[(1, *index)]

    for chunk in range(min(LOOKAHEAD, chunks)):
        send_own(chunk)

    for copy in locals_:
        copy.wait()
    carried[...] = jnp.zeros_like(carried)
    put(ib, invert(b_v[...]))
    put(ia, invert(a_v[...]))
    put(ph, p_v[...])
    put(pa, dot3(split(p_v[...].T), both(ia)))
    put(vp, dot3(both(pa), both(ph)))
    put(qt, q_v[...].T)
    put(bq, dot3(both(ib), split(q_v[...])))
    put(qw, dot3(both(qt), both(bq)))

    @pl.when(jnp.logical_not(has_prev))
    def _():
        blank = pltpu.make_async_copy(carried, earlier_ref, local_sem.at[0])
        blank.start()
        blank.wait()

    mixed[...] = jnp.zeros_like(mixed)

    @pl.when(jnp.logical_not(has_next))
    def _():
        follow[...] = jnp.zeros_like(follow)

    for source in range(n):
        @pl.when(source != me)
        def _(source=source):
            x_arrival(source).wait_recv()

        xt[:, source * tokens:(source + 1) * tokens] = xcols[source].T

    def mixed_in(chunk, next_parts):
        part = slice(chunk * width, (chunk + 1) * width)
        mixed[...] += dot3(split(dot3(both(ph), next_parts)), both(qt, part))

    def arrived(chunk):
        @pl.when(has_next)
        def _():
            g_copy(chunk).wait_recv()

        return split(follow[:, chunk * width:(chunk + 1) * width])

    def rows_of(ref, chunk):
        return both(ref, slice(chunk * width, (chunk + 1) * width))

    waiting = []
    for turn in range(chunks + n - 2):
        if turn + LOOKAHEAD < chunks:
            send_own(turn + LOOKAHEAD)
        relay(turn)
        chunk = turn - (n - 2)
        if chunk < 0:
            if waiting:
                waiting.pop(0)()
            continue
        part = slice(chunk * width, (chunk + 1) * width)
        right = call[:, :, part].reshape(n * tokens, width)
        grad[:, part] = dot(xt[...], right)

        @pl.when(has_prev)
        def _(chunk=chunk):
            g_copy(chunk).start()

        while waiting:
            waiting.pop(0)()
        carried[...] += dot3(split(dot3(both(pa), split(grad[:, part]))), rows_of(bq, chunk))
        if chunk > 0:
            after = arrived(chunk - 1)
            mixed_in(chunk - 1, after)
            carried[...] -= dot3(split(dot3(both(vp), after)), rows_of(qw, chunk - 1))

    last = chunks - 1
    after = arrived(last)
    half = split(dot3(both(vp), after))
    rows = slice(last * width, (last + 1) * width)
    for chunk in range(chunks):
        part = slice(chunk * width, (chunk + 1) * width)
        carried[:, part] -= dot3(half, both(qw, rows, part))

        @pl.when(has_next)
        def _(chunk=chunk):
            k_copy(chunk).start()

    mixed_in(last, after)
    coupled = split(grad[...] - mixed[...])
    scaled[...] = dot3(split(dot3(both(ia), coupled)), both(ib))
    result = pltpu.make_async_copy(scaled, scaled_ref, local_sem.at[0])
    result.start()
    for chunk in range(chunks):
        @pl.when(has_prev)
        def _(chunk=chunk):
            k_copy(chunk).wait_recv()

    result.wait()

    for d in range(n - 1, 0, -1):
        for target in (me + d, me - d):
            @pl.when((target >= 0) & (target < n))
            def _(target=target):
                x_copy(target).wait_send()
    for chunk in range(chunks):
        for step in (1, -1):
            for d in range(n):
                source = me - step * d

                @pl.when((source >= 0) & (source < n) & can_go(step))
                def _(source=source, step=step, chunk=chunk, d=d):
                    c_copy(source, chunk, step, d == 0).wait_send()

        @pl.when(has_prev)
        def _(chunk=chunk):
            g_copy(chunk).wait_send()

        @pl.when(has_next)
        def _(chunk=chunk):
            k_copy(chunk).wait_send()


def shards(layers, n, inputs, cotangents, input_factors, output_factors, input_coupling, output_coupling):
    tokens = inputs.shape[1]
    block = input_factors.shape[2]
    outc = cotangents.shape[2]
    chunks = outc // min(WIDTH, outc)
    dma = pltpu.SemaphoreType.DMA
    panel = pltpu.VMEM((block, outc), F32)
    scaled, earlier = pl.pallas_call(
        functools.partial(kernel, layers, n),
        out_shape=[pltpu.VMEM((block, outc), F32)] * 2,
        in_specs=[pl.BlockSpec(memory_space=pl.ANY)] * 6,
        out_specs=[pl.BlockSpec(memory_space=pltpu.VMEM)] * 2,
        scratch_shapes=[
            pltpu.VMEM((n, tokens, block), BF16),
            pltpu.VMEM((block, n * tokens), BF16),
            pltpu.VMEM((n, tokens, outc), BF16),
            pltpu.VMEM((block, block), F32),
            pltpu.VMEM((outc, outc), F32),
            pltpu.VMEM((block, block), F32),
            pltpu.VMEM((outc, outc), F32),
            pltpu.VMEM((2, block, block), BF16),
            pltpu.VMEM((2, outc, outc), BF16),
            pltpu.VMEM((2, block, block), BF16),
            pltpu.VMEM((2, block, block), BF16),
            pltpu.VMEM((2, block, block), BF16),
            pltpu.VMEM((2, outc, outc), BF16),
            pltpu.VMEM((2, outc, outc), BF16),
            pltpu.VMEM((2, outc, outc), BF16),
            panel, panel, panel, panel, panel,
            dma((6,)),
            dma((n,)), dma((n,)),
            dma((2, n, chunks)), dma((n, chunks)),
            dma((chunks,)), dma((chunks,)), dma((chunks,)), dma((chunks,)),
        ],
        compiler_params=pltpu.CompilerParams(
            collective_id=0, has_side_effects=True, vmem_limit_bytes=VMEM - 8 * block * outc - 65536),
    )(inputs, cotangents, input_factors, output_factors, input_coupling, output_coupling)
    return (scaled - earlier)[None]


def solution(mesh):
    in_specs = (
        P("pipe", "dp", None),
        P("pipe", "dp", None),
        P("pipe", "dp", None),
        P("pipe", None, None),
        P("pipe", "dp", None),
        P("pipe", None, None),
    )
    body = functools.partial(shards, mesh.shape["pipe"], mesh.shape["dp"])
    return jax.shard_map(body, mesh=mesh, in_specs=in_specs, out_specs=P("pipe", "dp", None), check_vma=False)
```
